768 devices in a mesh: rows: 12 (over z), cols: 8 (over y_hi, core), poles: 8 (over x, y_lo).
Axes of the slice: x: 4, y: 8 (y_hi: 4, y_lo: 2; y = y_hi * 2 + y_lo), z: 12, core: 2. Of those that a mesh axis runs over, the one named last changes fastest.
Arguments:
- inverse_grid: float32 [8, 12, 128, 8, 192], P('poles', 'rows', None, 'cols'), may hold values from -6 to 6
- factor_b: float32 [8, 12, 8, 16, 512], P('poles', 'rows', 'cols'), may hold values from -0.15625 to 0.15625
- factor_a: float32 [8, 12, 8, 16, 512], P('poles', 'rows', 'cols'), may hold values from -0.15625 to 0.15625
- coupling_a: float32 [8, 512, 512], P('poles'), may hold values from -0.25 to 0.25
- diag_inv_b: float32 [8, 512, 512], P('poles'), may hold values from -6 to 6
- diag_inv_a: float32 [8, 512, 512], P('poles'), may hold values from -6 to 6
- pole_weights: float32 [8], P('poles'), may hold values from 0.1 to 0.6
- structure: int32 [2, 12, 8], P(None, 'rows', 'cols'), may hold values 0 or 1
Outputs:
- density_panel: float32 [12, 8, 16, 512], P('rows', 'cols', None, 'poles')
- density_diag: float32 [512, 512], P('poles', 'cols')
The draws below stay inside these ranges and needn't reach their ends.
All inputs are finite; a program needn't handle non-finite values. No bound on the sum of `structure` on one device may be relied on, other than what follows from the above.
Results may differ from the reference program's by a relative error of at most 0.00008.
Values sent between devices are 32-bit elements; how exact they have to be, the bound alone decides.
A program may use at most 32 MiB of HBM per device.

```python
import jax
import jax.numpy as jnp
from jax import lax

SUPER_WIDTH = 512
BLOCK_ROWS = 16
ANCESTORS = 1536
POLES = 8
N_ROWS = 12
N_COLS = 8


def set_ends(drawn, own_key, least, top_value):
    index_at = [jax.random.randint(jax.random.fold_in(own_key, axis), (), 0, length) for axis, length in enumerate(drawn.shape)]
    widest = drawn.shape.index(max(drawn.shape))
    next_to = index_at[:widest] + [(index_at[widest] + 1) % drawn.shape[widest]] + index_at[widest + 1:]
    return drawn.at[tuple(index_at)].set(least).at[tuple(next_to)].set(top_value)


def block_levels(rng, extent, cuts, smallest, largest):
    gain, own = 1.0, jax.random.fold_in(rng, 6)
    for dim, blocks in cuts:
        steps = jnp.exp(jax.random.uniform(jax.random.fold_in(own, dim), (blocks,), jnp.float32, smallest / len(cuts), largest / len(cuts)))
        gain = gain * jnp.repeat(steps, extent[dim] // blocks).reshape([-1 if axis == dim else 1 for axis in range(len(extent))])
    return gain


def normal_values(rng, extent, deviation, limit, split=(), held_as=jnp.bfloat16):
    gain = block_levels(rng, extent, split, -0.22, 0.18) if split else 1.0
    values = jax.random.normal(rng, extent, jnp.float32) * deviation * gain
    return jnp.minimum(jnp.maximum(values, -limit), limit).astype(held_as)


def setup_inputs(seed: int = 0) -> dict:
    streams_of = jax.random.split(jax.random.key(seed), 9)
    inverse_grid = normal_values(streams_of[0], (POLES, N_ROWS, N_COLS * BLOCK_ROWS, N_COLS, N_ROWS * BLOCK_ROWS), 1.0, 6.0, ((0, 8), (1, 12), (3, 8)), jnp.float32)
    factor_b = normal_values(streams_of[1], (POLES, N_ROWS, N_COLS, BLOCK_ROWS, SUPER_WIDTH), ANCESTORS ** -0.5, 0.15625, ((0, 8), (1, 12), (2, 8)), jnp.float32)
    factor_a = normal_values(streams_of[2], (POLES, N_ROWS, N_COLS, BLOCK_ROWS, SUPER_WIDTH), ANCESTORS ** -0.5, 0.15625, ((0, 8), (1, 12), (2, 8)), jnp.float32)
    coupling_a = normal_values(streams_of[3], (POLES, SUPER_WIDTH, SUPER_WIDTH), SUPER_WIDTH ** -0.5, 0.25, ((0, 8),), jnp.float32)
    diag_inv_b = normal_values(streams_of[4], (POLES, SUPER_WIDTH, SUPER_WIDTH), 1.0, 6.0, ((0, 8),), jnp.float32)
    diag_inv_a = normal_values(streams_of[5], (POLES, SUPER_WIDTH, SUPER_WIDTH), 1.0, 6.0, ((0, 8),), jnp.float32)
    pole_weights = jnp.clip(0.1 + 0.5 * jax.random.uniform(streams_of[6], (POLES,), jnp.float32) ** block_levels(streams_of[6], (POLES,), ((0, 8),), -0.2, 0.2), 0.1, 0.6)
    structure = set_ends((jax.random.randint(streams_of[7], (2, N_ROWS, N_COLS), 0, 4) < 3).astype(jnp.int32), jax.random.fold_in(streams_of[7], 1), 0, 1)
    return dict(inverse_grid=inverse_grid, factor_b=factor_b, factor_a=factor_a, coupling_a=coupling_a, diag_inv_b=diag_inv_b, diag_inv_a=diag_inv_a, pole_weights=pole_weights, structure=structure)


def product(left, right):
    return jnp.dot(left, right, precision=lax.Precision.HIGHEST, preferred_element_type=jnp.float32)


def reference(inverse_grid, factor_b, factor_a, coupling_a, diag_inv_b, diag_inv_a, pole_weights, structure):
    kept_mask = structure.astype(jnp.float32)

    def one_pole(items):
        local_grid, rows_b, rows_a, coupling, inv_diag_b, inv_diag_a, weight = items
        full_inverse = local_grid.reshape(N_ROWS, N_COLS, BLOCK_ROWS, N_COLS, N_ROWS, BLOCK_ROWS)
        full_inverse = full_inverse.transpose(0, 1, 2, 4, 3, 5).reshape(ANCESTORS, ANCESTORS)
        panel_b = (rows_b * kept_mask[0][:, :, None, None]).reshape(ANCESTORS, SUPER_WIDTH)
        panel_a = (rows_a * kept_mask[1][:, :, None, None]).reshape(ANCESTORS, SUPER_WIDTH)
        inv_b = -product(full_inverse, panel_b)
        diag_b = inv_diag_b - product(panel_b.T, inv_b)
        inv_ab = -(product(diag_b, coupling) + product(inv_b.T, panel_a))
        inv_as = -(product(inv_b, coupling) + product(full_inverse, panel_a))
        diag_a = inv_diag_a - product(coupling.T, inv_ab) - product(panel_a.T, inv_as)
        return weight * inv_as, weight * diag_a

    panels, diags = lax.map(one_pole, (inverse_grid, factor_b, factor_a, coupling_a, diag_inv_b, diag_inv_a, pole_weights))
    density_panel = jnp.sum(panels, axis=0).reshape(N_ROWS, N_COLS, BLOCK_ROWS, SUPER_WIDTH)
    density_diag = jnp.sum(diags, axis=0)
    return density_panel, density_diag
```

```python
import jax
import jax.numpy as jnp
from jax import lax
from jax.experimental import pallas as pl
from jax.experimental.pallas import tpu as pltpu
from jax.sharding import PartitionSpec as P

MESH = pl.DeviceIdType.MESH
F32 = jnp.float32
WIDTH, BLOCK = 512, 16
NR, NC, NP = 12, 8, 8
CHUNK = WIDTH // NP
LANES = 2 * CHUNK
ROWS = NC * BLOCK
PER_CORE = NC // 2
HALF = CHUNK // 2
RIGHT_REACH = (6, 5)
LEFT_REACH = (5, 6)


def dot(left, right, contract=((1,), (0,))):
    return lax.dot_general(
        left, right, (contract, ((), ())), precision=lax.Precision.HIGH, preferred_element_type=F32
    )


def swap_halves(x):
    return pltpu.roll(x, CHUNK, axis=x.ndim - 1)


def low_lanes(shape):
    return lax.broadcasted_iota(jnp.int32, shape, len(shape) - 1) < CHUNK


def pack(top, bottom):
    return jnp.where(low_lanes(top.shape), top, swap_halves(bottom))


def unpack(x):
    return jnp.concatenate([x, swap_halves(x)], axis=0)


def remote(src, dst, send, recv, to):
    return pltpu.make_async_remote_copy(
        src_ref=src, dst_ref=dst, send_sem=send, recv_sem=recv, device_id=to, device_id_type=MESH
    )


def kernel(
    g_hbm, lb_hbm, la_hbm, c_hbm, db_hbm, da_hbm, weight_s, keep_s,
    panel_ref, diag_ref,
    gt, lb, la, coup, dbk, dak, own, zbuf, rows, wsend, wrecv, fsend, frecv, qsend, qrecv, tsend, trecv,
    load_sem, g_send, g_recv, z_send, z_recv, hop_send, pair_send, pair_recv, r_send, r_recv,
    w_send, w_recv, f_send, f_recv, q_send, q_recv, t_send, t_recv,
):
    u, v, p = lax.axis_index("rows"), lax.axis_index("cols"), lax.axis_index("poles")
    h, chip = lax.rem(v, 2), v // 2
    mate = chip * 2 + 1 - h
    part = jnp.minimum(u, NP - 1)

    loads = [
        pltpu.make_async_copy(lb_hbm, lb, load_sem.at[0]),
        pltpu.make_async_copy(la_hbm, la, load_sem.at[1]),
        pltpu.make_async_copy(c_hbm, coup, load_sem.at[2]),
        pltpu.make_async_copy(g_hbm, gt.at[h], load_sem.at[3]),
        pltpu.make_async_copy(db_hbm.at[pl.ds(part * CHUNK, CHUNK)], dbk, load_sem.at[4]),
        pltpu.make_async_copy(da_hbm.at[pl.ds(v * CHUNK, CHUNK)], dak, load_sem.at[5]),
    ]
    for copy in loads:
        copy.start()

    barrier = pltpu.get_barrier_semaphore()

    def greet(to):
        pl.semaphore_signal(barrier, inc=1, device_id=to, device_id_type=MESH)

    for step in (1, NR - 1):
        greet((lax.rem(u + step, NR), mate, p))
    for step in range(1, NR):
        greet((lax.rem(u + step, NR), v, p))
    for step in range(1, NC):
        greet((u, lax.rem(v + step, NC), p))
        greet((u, v, lax.rem(p + step, NP)))
    for q in range(NP):

        @pl.when(jnp.logical_not(jnp.logical_and(v == p, p == q)))
        def _():
            greet((u, p, q))

    weight = weight_s[0]
    keep_b = keep_s[0].astype(F32)
    keep_a = keep_s[1].astype(F32)
    for copy in loads[:3]:
        copy.wait()
    panel_a = la[...] * keep_a
    panel_n = dot(lb[...] * keep_b, coup[...])
    for pair in range(NC // 2):
        a, n = (x[:, pair * LANES : (pair + 1) * LANES] for x in (panel_a, panel_n))
        own[2 * pair] = pack(a, n)
        own[2 * pair + 1] = jnp.where(low_lanes(a.shape), swap_halves(a), n)
    loads[3].wait()

    expected = 2 + (NR - 1) + (NC - 1) + (NP - 1) + NP
    pl.semaphore_wait(barrier, expected - (v == p).astype(jnp.int32))

    right, left = lax.rem(u + 1, NR), lax.rem(u + NR - 1, NR)
    mine = own.at[pl.ds(h * PER_CORE, PER_CORE)]
    others = own.at[pl.ds((1 - h) * PER_CORE, PER_CORE)]
    sent = []

    def send(copy):
        copy.start()
        sent.append(copy)

    for d, to in ((0, right), (1, left)):
        send(remote(mine, zbuf.at[h, u], hop_send.at[d, 0], z_recv.at[d, 0, h], (to, v, p)))
        send(remote(others, zbuf.at[h, u], hop_send.at[d, 1], z_recv.at[d, 0, h], (to, mate, p)))
    send(remote(others, zbuf.at[h, u], pair_send, pair_recv, (u, mate, p)))
    send(remote(gt.at[h], gt.at[h], g_send, g_recv, (u, mate, p)))
    for step in range(1, NC):
        to = lax.rem(v + step, NC)
        send(remote(own, rows.at[v], r_send.at[step - 1], r_recv.at[v], (u, to, p)))
    zbuf[h, u] = own[pl.ds(h * PER_CORE, PER_CORE)]
    rows[v] = own[...]

    for copy in loads[4:]:
        copy.wait()
    columns = coup[:, pl.ds(pl.multiple_of(chip * LANES, LANES), LANES)]
    inner = dot(dbk[...], columns)
    inner = jnp.where(h == 0, inner, swap_halves(inner))
    inner = inner * (weight * (u < NP).astype(F32))
    fixed = dot(inner, coup[pl.ds(part * CHUNK, CHUNK), :], ((0,), (0,)))[:CHUNK]

    def arrived(buf, sem):
        remote(buf, buf, pair_send, sem, (u, mate, p)).wait_recv()

    for hop in range(1, NR // 2 + 1):
        for s in range(2):
            for d, (reach, to) in enumerate(((RIGHT_REACH, right), (LEFT_REACH, left))):
                if hop > reach[s]:
                    continue
                origin = lax.rem(u + (NR - hop if d == 0 else hop), NR)
                slot = zbuf.at[s, origin]
                arrived(slot, z_recv.at[d, hop - 1, s])
                if hop < reach[s]:
                    send(remote(slot, slot, z_send.at[d, hop - 1, s], z_recv.at[d, hop, s], (to, v, p)))
        if hop == 1:
            arrived(zbuf.at[1 - h, u], pair_recv)
            arrived(gt.at[1 - h], g_recv)
            inverse = gt[...].reshape(2 * NR * BLOCK, ROWS).T

    for ch in range(PER_CORE):
        gathered = zbuf[:, :, ch].reshape(2 * NR * BLOCK, LANES)
        wsend[ch] = dot(inverse, gathered)
        dest = h * PER_CORE + ch

        @pl.when(dest == v)
        def _():
            wrecv[chip] = wsend[ch]

        @pl.when(dest != v)
        def _():
            remote(wsend.at[ch], wrecv.at[chip], w_send.at[ch], w_recv.at[chip], (u, dest, p)).start()

    for step in range(1, NC):
        source = lax.rem(v + step, NC)
        arrived(rows.at[source], r_recv.at[source])
    for k in range(NC // 2):

        @pl.when(2 * k + v // PER_CORE != v)
        def _():
            arrived(wrecv.at[k], w_recv.at[k])

    both = (wrecv[0] + wrecv[1]) + (wrecv[2] + wrecv[3])
    panel = ((swap_halves(both) - both) * weight).reshape(NC, BLOCK, LANES)
    panel = pack(panel[:, : BLOCK // 2], panel[:, BLOCK // 2 :])
    turned = (both * weight).T
    for a in range(NP):
        terms = dot(turned, rows[:, a].reshape(ROWS, LANES))
        top, bottom = terms[:CHUNK], terms[CHUNK:]
        pair = slice(a // 2 * LANES, (a // 2 + 1) * LANES)
        here, block = fixed[:, pair], dak[:, pair]
        if a % 2:
            here, block = swap_halves(here), swap_halves(block)
        first = (top - bottom) + swap_halves(bottom) + here
        second = block * (weight * (u == a).astype(F32)) - bottom
        fsend[a] = pack(first[:HALF], first[HALF:])
        qsend[a, :HALF] = pack(second[:HALF], second[HALF:])
        qsend[a, HALF:] = panel[a]

        @pl.when(a == p)
        def _():
            frecv[p] = fsend[a]

        @pl.when(a != p)
        def _():
            remote(fsend.at[a], frecv.at[p], f_send.at[a], f_recv.at[p], (u, v, a)).start()

        mine_too = jnp.logical_and(v == p, a == v)

        @pl.when(mine_too)
        def _():
            qrecv[p] = qsend[a]

        @pl.when(jnp.logical_not(mine_too))
        def _():
            remote(qsend.at[a], qrecv.at[p], q_send.at[a], q_recv.at[p], (u, a, v)).start()

    for q in range(NP):

        @pl.when(q != p)
        def _():
            arrived(frecv.at[q], f_recv.at[q])

        @pl.when(jnp.logical_not(jnp.logical_and(v == p, q == p)))
        def _():
            arrived(qrecv.at[q], q_recv.at[q])

    first, second = frecv[0], qrecv[0]
    for q in range(1, NP):
        first, second = first + frecv[q], second + qrecv[q]
    first = unpack(first)
    first = jnp.concatenate([first, first], axis=0).T[:CHUNK]
    total = first + unpack(second[:HALF])
    tsend[...] = pack(total[:HALF], total[HALF:])
    for step in range(1, NR):
        to = lax.rem(u + step, NR)
        send(remote(tsend, trecv.at[u], t_send.at[step - 1], t_recv.at[u], (to, v, p)))
    trecv[u] = tsend[...]
    panel_ref[...] = unpack(second[HALF:])[:, :CHUNK]

    for step in range(1, NR):
        source = lax.rem(u + step, NR)
        arrived(trecv.at[source], t_recv.at[source])
    total = trecv[0]
    for k in range(1, NR):
        total = total + trecv[k]
    diag_ref[...] = unpack(total)[:, :CHUNK]

    for copy in sent:
        copy.wait_send()
    for ch in range(PER_CORE):

        @pl.when(h * PER_CORE + ch != v)
        def _():
            remote(wsend.at[ch], wsend.at[ch], w_send.at[ch], w_recv.at[0], (u, mate, p)).wait_send()

    for a in range(NP):

        @pl.when(a != p)
        def _():
            remote(fsend.at[a], fsend.at[a], f_send.at[a], f_recv.at[0], (u, mate, p)).wait_send()

        @pl.when(jnp.logical_not(jnp.logical_and(v == p, a == v)))
        def _():
            remote(qsend.at[a], qsend.at[a], q_send.at[a], q_recv.at[0], (u, mate, p)).wait_send()


def shards(
    inverse_grid, factor_b, factor_a, coupling_a, diag_inv_b, diag_inv_a, pole_weights, structure
):
    hbm = pl.BlockSpec(memory_space=pl.ANY)
    smem = pl.BlockSpec(memory_space=pltpu.SMEM)
    vmem = pl.BlockSpec(memory_space=pltpu.VMEM)
    dma = pltpu.SemaphoreType.DMA
    panel, diag = pl.pallas_call(
        kernel,
        out_shape=(
            jax.ShapeDtypeStruct((BLOCK, CHUNK), F32),
            jax.ShapeDtypeStruct((CHUNK, CHUNK), F32),
        ),
        in_specs=[hbm] * 6 + [smem] * 2,
        out_specs=(vmem, vmem),
        scratch_shapes=[
            pltpu.VMEM((2, NR * BLOCK, ROWS), F32),
            pltpu.VMEM((BLOCK, WIDTH), F32),
            pltpu.VMEM((BLOCK, WIDTH), F32),
            pltpu.VMEM((WIDTH, WIDTH), F32),
            pltpu.VMEM((CHUNK, WIDTH), F32),
            pltpu.VMEM((CHUNK, WIDTH), F32),
            pltpu.VMEM((NC, BLOCK, LANES), F32),
            pltpu.VMEM((2, NR, PER_CORE, BLOCK, LANES), F32),
            pltpu.VMEM((NC, NC, BLOCK, LANES), F32),
            pltpu.VMEM((PER_CORE, ROWS, LANES), F32),
            pltpu.VMEM((NC // 2, ROWS, LANES), F32),
            pltpu.VMEM((NP, HALF, LANES), F32),
            pltpu.VMEM((NP, HALF, LANES), F32),
            pltpu.VMEM((NP, HALF + BLOCK // 2, LANES), F32),
            pltpu.VMEM((NP, HALF + BLOCK // 2, LANES), F32),
            pltpu.VMEM((HALF, LANES), F32),
            pltpu.VMEM((NR, HALF, LANES), F32),
            dma((6,)), dma, dma, dma((2, 6, 2)), dma((2, 6, 2)), dma((2, 2)), dma, dma,
            dma((NC - 1,)), dma((NC,)), dma((PER_CORE,)), dma((NC // 2,)),
            dma((NP,)), dma((NP,)), dma((NP,)), dma((NP,)), dma((NR - 1,)), dma((NR,)),
        ],
        compiler_params=pltpu.CompilerParams(collective_id=0, has_side_effects=True),
    )(
        inverse_grid[0, 0, :, 0, :].T,
        factor_b[0, 0, 0],
        factor_a[0, 0, 0],
        coupling_a[0],
        diag_inv_b[0],
        diag_inv_a[0],
        pole_weights,
        structure[:, 0, 0],
    )
    return panel[None, None], diag


def solution(mesh):
    in_specs = (
        P("poles", "rows", None, "cols", None),
        P("poles", "rows", "cols", None, None),
        P("poles", "rows", "cols", None, None),
        P("poles", None, None),
        P("poles", None, None),
        P("poles", None, None),
        P("poles"),
        P(None, "rows", "cols"),
    )
    out_specs = (P("rows", "cols", None, "poles"), P("poles", "cols"))
    return jax.shard_map(shards, mesh=mesh, in_specs=in_specs, out_specs=out_specs, check_vma=False)
```

```python
import jax
import jax.numpy as jnp
from jax import lax
from jax.experimental import pallas as pl
from jax.experimental.pallas import tpu as pltpu
from jax.sharding import PartitionSpec as P

MESH = pl.DeviceIdType.MESH
F32 = jnp.float32
WIDTH, BLOCK = 512, 16
NR, NC, NP = 12, 8, 8
CHUNK = WIDTH // NP
LANES = 2 * CHUNK
ROWS = NC * BLOCK
PER_CORE = NC // 2
HALF = CHUNK // 2
DIRECT = 2
REACH = ((6, 5), (5, 6))


def dot(left, right, contract=((1,), (0,))):
    return lax.dot_general(
        left, right, (contract, ((), ())), precision=lax.Precision.HIGH, preferred_element_type=F32
    )


def swap_halves(x):
    return pltpu.roll(x, CHUNK, axis=x.ndim - 1)


def low_lanes(shape):
    return lax.broadcasted_iota(jnp.int32, shape, len(shape) - 1) < CHUNK


def pack(top, bottom):
    return jnp.where(low_lanes(top.shape), top, swap_halves(bottom))


def unpack(x):
    return jnp.concatenate([x, swap_halves(x)], axis=0)


def remote(src, dst, send, recv, to):
    return pltpu.make_async_remote_copy(
        src_ref=src, dst_ref=dst, send_sem=send, recv_sem=recv, device_id=to, device_id_type=MESH
    )


def kernel(
    g_hbm, lb_hbm, la_hbm, c_hbm, db_hbm, da_hbm, weight_hbm, keep_hbm,
    panel_ref, diag_ref,
    weight_s, keep_s, gt, lb, la, coup, dbk, dak, fixed, own, zbuf, rows, turned, wsend, wrecv, fsend, frecv, qsend, qrecv, tsend, trecv,
    load_sem, scalar_sem, g_send, g_recv, z_send, z_recv, hop_send, pair_send, pair_recv, r_send, r_recv,
    w_send, w_recv, f_send, f_recv, q_send, q_recv, t_send, t_recv,
):
    u, v, p = lax.axis_index("rows"), lax.axis_index("cols"), lax.axis_index("poles")
    h, chip = lax.rem(v, 2), v // 2
    mate = chip * 2 + 1 - h
    part = jnp.minimum(u, NP - 1)

    loads = [
        pltpu.make_async_copy(lb_hbm, lb, load_sem.at[0]),
        pltpu.make_async_copy(la_hbm, la, load_sem.at[1]),
        pltpu.make_async_copy(c_hbm, coup, load_sem.at[2]),
        pltpu.make_async_copy(g_hbm, gt.at[h], load_sem.at[3]),
        pltpu.make_async_copy(db_hbm.at[pl.ds(part * CHUNK, CHUNK)], dbk, load_sem.at[4]),
        pltpu.make_async_copy(da_hbm.at[pl.ds(part * CHUNK, CHUNK), pl.ds(pl.multiple_of(chip * LANES, LANES), LANES)], dak, load_sem.at[5]),
    ]
    scalars = [
        pltpu.make_async_copy(weight_hbm, weight_s, scalar_sem.at[0]),
        pltpu.make_async_copy(keep_hbm, keep_s, scalar_sem.at[1]),
    ]
    for copy in loads[:3] + scalars + loads[3:]:
        copy.start()

    barrier = pltpu.get_barrier_semaphore()

    def greet(to):
        pl.semaphore_signal(barrier, inc=1, device_id=to, device_id_type=MESH)

    for step in range(1, DIRECT + 1):
        for to in (lax.rem(u + step, NR), lax.rem(u + NR - step, NR)):
            greet((to, v, p))
            greet((to, mate, p))
    for step in range(1, NC):
        greet((u, lax.rem(v + step, NC), p))
        greet((u, v, lax.rem(p + step, NP)))
    for copy in scalars + loads[:3]:
        copy.wait()
    weight = weight_s[0]
    keep_b = keep_s[0].astype(F32)
    keep_a = keep_s[1].astype(F32)
    panel_a = la[...] * keep_a
    panel_n = dot(lb[...] * keep_b, coup[...])
    for pair in range(NC // 2):
        a, n = (x[:, pair * LANES : (pair + 1) * LANES] for x in (panel_a, panel_n))
        own[2 * pair] = pack(a, n)
        own[2 * pair + 1] = jnp.where(low_lanes(a.shape), swap_halves(a), n)
    loads[3].wait()

    pl.semaphore_wait(barrier, 4 * DIRECT + (NC - 1) + (NP - 1))

    mine = own.at[pl.ds(h * PER_CORE, PER_CORE)]
    others = own.at[pl.ds((1 - h) * PER_CORE, PER_CORE)]
    sent = []

    def send(copy):
        copy.start()
        sent.append(copy)

    def along(d, hops):
        return lax.rem(u + (hops if d == 0 else NR - hops), NR)

    for hops in range(DIRECT, 0, -1):
        for d in range(2):
            to, send_sem, recv_sem = along(d, hops), hop_send.at[d, hops - 1], z_recv.at[d, hops - 1, h]
            send(remote(mine, zbuf.at[h, u], send_sem.at[0], recv_sem, (to, v, p)))
            send(remote(others, zbuf.at[h, u], send_sem.at[1], recv_sem, (to, mate, p)))
        if hops == DIRECT:
            send(remote(others, zbuf.at[h, u], pair_send, pair_recv, (u, mate, p)))
            send(remote(gt.at[h], gt.at[h], g_send, g_recv, (u, mate, p)))
    for step in range(1, NC // 2):
        to = lax.rem(v + 2 * step, NC)
        send(remote(own, rows.at[v], r_send.at[step], r_recv.at[v], (u, to, p)))
    send(remote(own, rows.at[v], r_send.at[0], r_recv.at[v], (u, mate, p)))
    zbuf[h, u] = own[pl.ds(h * PER_CORE, PER_CORE)]
    rows[v] = own[...]

    for copy in loads[4:]:
        copy.wait()
    scale = weight * (u < NP).astype(F32)
    columns = coup[:, pl.ds(pl.multiple_of(chip * LANES, LANES), LANES)]
    inner = dot(dbk[...], columns)
    inner = jnp.where(h == 0, inner, swap_halves(inner)) * scale
    fixed[...] = dot(coup[pl.ds(part * CHUNK, CHUNK), :], inner, ((0,), (0,)))
    block = jnp.where(h == 0, dak[...], swap_halves(dak[...])) * scale
    fixed[pl.ds(part * CHUNK, CHUNK)] += block

    def arrived(buf, sem):
        remote(buf, buf, pair_send, sem, (u, mate, p)).wait_recv()

    def piece(d, hops, s):
        slot = zbuf.at[s, along(1 - d, hops)]
        arrived(slot, z_recv.at[d, hops - 1, s])
        return slot

    for past in range(DIRECT, NR // 2, DIRECT):
        for s in range(2):
            for d in range(2):
                slot = piece(d, past, s)
                for more in range(min(DIRECT, REACH[d][s] - past), 0, -1):
                    end = past + more - 1
                    send(remote(slot, slot, z_send.at[d, s, end], z_recv.at[d, end, s], (along(d, more), v, p)))
    arrived(zbuf.at[1 - h, u], pair_recv)
    arrived(gt.at[1 - h], g_recv)
    inverse = gt[...].reshape(2 * NR * BLOCK, ROWS).T
    for step in range(1, NC // 2):
        source = lax.rem(v + 2 * step, NC)
        block = rows.at[source]
        arrived(block, r_recv.at[source])
        send(remote(block, block, r_send.at[NC // 2 - 1 + step], r_recv.at[source], (u, mate, p)))
    for step in range(NC // 2):
        source = lax.rem(mate + 2 * step, NC)
        arrived(rows.at[source], r_recv.at[source])
    for a in range(NP):
        turned[a * LANES : (a + 1) * LANES] = rows[:, a].reshape(ROWS, LANES).T
    for hops in range(1, NR // 2 + 1):
        for s in range(2):
            for d in range(2):
                if (hops % DIRECT or hops >= NR // 2) and hops <= REACH[d][s]:
                    piece(d, hops, s)

    for ch in range(PER_CORE):
        gathered = zbuf[:, :, ch].reshape(2 * NR * BLOCK, LANES)
        wsend[ch] = dot(inverse, gathered)
        dest = h * PER_CORE + ch

        @pl.when(dest == v)
        def _():
            wrecv[chip] = wsend[ch]

        @pl.when(dest != v)
        def _():
            remote(wsend.at[ch], wrecv.at[chip], w_send.at[ch], w_recv.at[chip], (u, dest, p)).start()

    for k in range(NC // 2):

        @pl.when(2 * k + v // PER_CORE != v)
        def _():
            arrived(wrecv.at[k], w_recv.at[k])

    both = (wrecv[0] + wrecv[1]) + (wrecv[2] + wrecv[3])
    panel = ((swap_halves(both) - both) * weight).reshape(NC, BLOCK, LANES)
    panel = pack(panel[:, : BLOCK // 2], panel[:, BLOCK // 2 :])
    both = both * weight
    quarter = NP // 2
    terms = []
    for half in range(2):
        out = dot(turned[half * quarter * LANES : (half + 1) * quarter * LANES], both)
        for a in range(half * quarter, (half + 1) * quarter):
            at = (a - half * quarter) * LANES
            top, bottom = out[at : at + CHUNK], out[at + CHUNK : at + LANES]
            terms.append((top, bottom))
            qsend[a, :HALF] = jnp.where(low_lanes((HALF, LANES)), swap_halves(top[:HALF]), top[HALF:])
            qsend[a, HALF:] = panel[a]
            to_me = jnp.logical_and(v == p, a == v)

            @pl.when(to_me)
            def _():
                qrecv[p] = qsend[a]

            @pl.when(jnp.logical_not(to_me))
            def _():
                remote(qsend.at[a], qrecv.at[p], q_send.at[a], q_recv.at[p], (u, a, v)).start()

    for a, (top, bottom) in enumerate(terms):
        first = (top - swap_halves(top)) + swap_halves(bottom) + fixed[a * CHUNK : (a + 1) * CHUNK]
        fsend[a] = pack(first[:HALF], first[HALF:])

        @pl.when(a == p)
        def _():
            frecv[p] = fsend[a]

        @pl.when(a != p)
        def _():
            remote(fsend.at[a], frecv.at[p], f_send.at[a], f_recv.at[p], (u, v, a)).start()

    for q in range(NP):

        @pl.when(q != p)
        def _():
            arrived(frecv.at[q], f_recv.at[q])

        @pl.when(jnp.logical_not(jnp.logical_and(v == p, q == p)))
        def _():
            arrived(qrecv.at[q], q_recv.at[q])

    first, second = frecv[0], qrecv[0]
    for q in range(1, NP):
        first, second = first + frecv[q], second + qrecv[q]
    back = unpack(second[:HALF])
    back = jnp.concatenate([back, back], axis=0).T[:CHUNK]
    total = unpack(first) - back
    tsend[...] = pack(total[:HALF], total[HALF:])
    for step in range(1, NR):
        to = lax.rem(u + step, NR)
        send(remote(tsend, trecv.at[u], t_send.at[step - 1], t_recv.at[u], (to, v, p)))
    trecv[u] = tsend[...]
    panel_ref[...] = unpack(second[HALF:])[:, :CHUNK]

    for step in range(1, NR):
        source = lax.rem(u + step, NR)
        arrived(trecv.at[source], t_recv.at[source])
    total = trecv[0]
    for k in range(1, NR):
        total = total + trecv[k]
    diag_ref[...] = unpack(total)[:, :CHUNK]

    for copy in sent:
        copy.wait_send()
    for ch in range(PER_CORE):

        @pl.when(h * PER_CORE + ch != v)
        def _():
            remote(wsend.at[ch], wsend.at[ch], w_send.at[ch], w_recv.at[0], (u, mate, p)).wait_send()

    for a in range(NP):

        @pl.when(a != p)
        def _():
            remote(fsend.at[a], fsend.at[a], f_send.at[a], f_recv.at[0], (u, mate, p)).wait_send()

        @pl.when(jnp.logical_not(jnp.logical_and(v == p, a == v)))
        def _():
            remote(qsend.at[a], qsend.at[a], q_send.at[a], q_recv.at[0], (u, mate, p)).wait_send()


def shards(
    inverse_grid, factor_b, factor_a, coupling_a, diag_inv_b, diag_inv_a, pole_weights, structure
):
    hbm = pl.BlockSpec(memory_space=pltpu.HBM)
    vmem = pl.BlockSpec(memory_space=pltpu.VMEM)
    dma = pltpu.SemaphoreType.DMA
    panel, diag = pl.pallas_call(
        kernel,
        out_shape=(
            pltpu.VMEM((BLOCK, CHUNK), F32),
            pltpu.VMEM((CHUNK, CHUNK), F32),
        ),
        in_specs=[hbm] * 8,
        out_specs=(vmem, vmem),
        scratch_shapes=[
            pltpu.SMEM((1,), F32),
            pltpu.SMEM((2,), jnp.int32),
            pltpu.VMEM((2, NR * BLOCK, ROWS), F32),
            pltpu.VMEM((BLOCK, WIDTH), F32),
            pltpu.VMEM((BLOCK, WIDTH), F32),
            pltpu.VMEM((WIDTH, WIDTH), F32),
            pltpu.VMEM((CHUNK, WIDTH), F32),
            pltpu.VMEM((CHUNK, LANES), F32),
            pltpu.VMEM((WIDTH, LANES), F32),
            pltpu.VMEM((NC, BLOCK, LANES), F32),
            pltpu.VMEM((2, NR, PER_CORE, BLOCK, LANES), F32),
            pltpu.VMEM((NC, NC, BLOCK, LANES), F32),
            pltpu.VMEM((NP * LANES, ROWS), F32),
            pltpu.VMEM((PER_CORE, ROWS, LANES), F32),
            pltpu.VMEM((NC // 2, ROWS, LANES), F32),
            pltpu.VMEM((NP, HALF, LANES), F32),
            pltpu.VMEM((NP, HALF, LANES), F32),
            pltpu.VMEM((NP, HALF + BLOCK // 2, LANES), F32),
            pltpu.VMEM((NP, HALF + BLOCK // 2, LANES), F32),
            pltpu.VMEM((HALF, LANES), F32),
            pltpu.VMEM((NR, HALF, LANES), F32),
            dma((6,)), dma((2,)), dma, dma, dma((2, 2, NR // 2)), dma((2, NR // 2, 2)), dma((2, DIRECT, 2)), dma, dma,
            dma((NC - 1,)), dma((NC,)), dma((PER_CORE,)), dma((NC // 2,)),
            dma((NP,)), dma((NP,)), dma((NP,)), dma((NP,)), dma((NR - 1,)), dma((NR,)),
        ],
        compiler_params=pltpu.CompilerParams(collective_id=0, has_side_effects=True),
    )(
        inverse_grid[0, 0, :, 0, :].T,
        factor_b[0, 0, 0],
        factor_a[0, 0, 0],
        coupling_a[0],
        diag_inv_b[0],
        diag_inv_a[0],
        pole_weights,
        structure[:, 0, 0],
    )
    return panel[None, None], diag


def solution(mesh):
    in_specs = (
        P("poles", "rows", None, "cols", None),
        P("poles", "rows", "cols", None, None),
        P("poles", "rows", "cols", None, None),
        P("poles", None, None),
        P("poles", None, None),
        P("poles", None, None),
        P("poles"),
        P(None, "rows", "cols"),
    )
    out_specs = (P("rows", "cols", None, "poles"), P("poles", "cols"))
    return jax.shard_map(shards, mesh=mesh, in_specs=in_specs, out_specs=out_specs, check_vma=False)
```

```python
import jax
import jax.numpy as jnp
from jax import lax
from jax.experimental import pallas as pl
from jax.experimental.pallas import tpu as pltpu
from jax.sharding import PartitionSpec as P

MESH = pl.DeviceIdType.MESH
F32 = jnp.float32
WIDTH, BLOCK = 512, 16
NR, NC, NP = 12, 8, 8
CHUNK = WIDTH // NP
LANES = 2 * CHUNK
ROWS = NC * BLOCK
HALF = CHUNK // 2
STRIDE = 2
REACH = ((6, 5), (5, 6))
GROUP = NC // 2
FAR_FIRST = sorted(range(1, NR), key=lambda step: -min(step, NR - step))
REACH = ((6, 5), (5, 6))


def dot(left, right, contract=((1,), (0,))):
    return lax.dot_general(
        left, right, (contract, ((), ())), precision=lax.Precision.HIGH, preferred_element_type=F32
    )


def swap_halves(x):
    return pltpu.roll(x, CHUNK, axis=x.ndim - 1)


def low_lanes(shape):
    return lax.broadcasted_iota(jnp.int32, shape, len(shape) - 1) < CHUNK


def pack(top, bottom):
    return jnp.where(low_lanes(top.shape), top, swap_halves(bottom))


def unpack(x):
    return jnp.concatenate([x, swap_halves(x)], axis=0)


def remote(src, dst, send, recv, to):
    return pltpu.make_async_remote_copy(
        src_ref=src, dst_ref=dst, send_sem=send, recv_sem=recv, device_id=to, device_id_type=MESH
    )


def kernel(
    g_hbm, lb_hbm, la_hbm, c_hbm, db_hbm, da_hbm, weight_hbm, keep_hbm,
    panel_ref, diag_ref,
    weight_s, keep_s, gt, lb, la, coup, dbk, dak, fixed, own, zbuf, rows, inverse, turned, terms, panel_out,
    fsend, frecv, qsend, qrecv, tsend, trecv,
    load_sem, late_sem, tile_send, tile_recv, g_send, g_recv, g_pass, z_send, z_pass, z_near, z_far,
    r_send, r_recv, r_pass, f_send, f_recv, q_send, q_recv, t_send, t_recv,
):
    u, v, p = lax.axis_index("rows"), lax.axis_index("cols"), lax.axis_index("poles")
    h, chip = lax.rem(v, 2), v // 2
    mate = chip * 2 + 1 - h
    part = jnp.minimum(u, NP - 1)

    lanes = pl.ds(pl.multiple_of(chip * LANES, LANES), LANES)
    loads = [
        pltpu.make_async_copy(lb_hbm, lb, load_sem.at[0]),
        pltpu.make_async_copy(la_hbm, la, load_sem.at[1]),
        pltpu.make_async_copy(c_hbm, coup, load_sem.at[2]),
        pltpu.make_async_copy(weight_hbm, weight_s, load_sem.at[3]),
        pltpu.make_async_copy(keep_hbm, keep_s, load_sem.at[4]),
    ]
    later = [
        pltpu.make_async_copy(g_hbm, gt.at[v], late_sem.at[0]),
        pltpu.make_async_copy(db_hbm.at[pl.ds(part * CHUNK, CHUNK)], dbk, late_sem.at[1]),
        pltpu.make_async_copy(da_hbm.at[pl.ds(part * CHUNK, CHUNK), lanes], dak, late_sem.at[2]),
    ]
    for copy in loads + later:
        copy.start()

    barrier = pltpu.get_barrier_semaphore()

    def greet(to):
        pl.semaphore_signal(barrier, inc=1, device_id=to, device_id_type=MESH)

    for step in range(1, STRIDE + 1):
        greet((lax.rem(u + step, NR), v, p))
        greet((lax.rem(u + NR - step, NR), v, p))
    for step in range(1, NC):
        greet((u, lax.rem(v + step, NC), p))
        greet((u, v, lax.rem(p + step, NP)))

    for copy in loads:
        copy.wait()
    weight = weight_s[0]
    keep_b = keep_s[0].astype(F32)
    keep_a = keep_s[1].astype(F32)
    panel_a = la[...] * keep_a
    panel_n = dot(lb[...] * keep_b, coup[...])
    for pair in range(NC // 2):
        a, n = (x[:, pair * LANES : (pair + 1) * LANES] for x in (panel_a, panel_n))
        own[2 * pair] = pack(a, n)
        own[2 * pair + 1] = jnp.where(low_lanes(a.shape), swap_halves(a), n)
    pl.semaphore_wait(barrier, 2 * STRIDE + (NC - 1) + (NP - 1))

    def along(d, hops):
        return lax.rem(u + (hops if d == 0 else NR - hops), NR)

    def slot(d, hops):
        return min(2 * hops - 1 + d, NR - 1)

    def arrived(buf, sem):
        remote(buf, buf, tile_send, sem, (u, mate, p)).wait_recv()

    def left(buf, sem):
        remote(buf, buf, sem, tile_recv, (u, mate, p)).wait_send()

    for step in (4, 5, 3, 2, 6, 7, 1):
        to = lax.rem(v + step, NC)
        remote(own.at[to], zbuf.at[0, v], tile_send, tile_recv, (u, to, p)).start()
    zbuf[0, v] = own[v]
    rows[v] = own[...]
    later[0].wait()
    for step in (4, 2, 6):
        remote(gt.at[v], gt.at[v], g_send, g_recv, (u, lax.rem(v + step, NC), p)).start()
    remote(gt.at[v], gt.at[v], g_send, g_pass, (u, mate, p)).start()
    for step in (4, 2, 6):
        remote(own, rows.at[v], r_send, r_recv, (u, lax.rem(v + step, NC), p)).start()
    remote(own, rows.at[v], r_send, r_pass, (u, mate, p)).start()

    for copy in later[1:]:
        copy.wait()
    scale = weight * (u < NP).astype(F32)
    inner = dot(dbk[...], coup[:, lanes])
    inner = jnp.where(h == 0, inner, swap_halves(inner)) * scale
    fixed[...] = dot(coup[pl.ds(part * CHUNK, CHUNK), :], inner, ((0,), (0,)))
    block = jnp.where(h == 0, dak[...], swap_halves(dak[...])) * scale
    fixed[pl.ds(part * CHUNK, CHUNK)] += block

    arrived(zbuf.at[0, : NC - 1], tile_recv)
    for g in range(2):
        piece = pl.ds(g * GROUP, GROUP)
        for d in range(2):
            to = (along(d, STRIDE), v, p)
            remote(zbuf.at[0, piece], zbuf.at[slot(d, STRIDE), piece], z_send, z_pass.at[d, 0, g], to).start()
    for d in range(2):
        remote(zbuf.at[0], zbuf.at[slot(d, 1)], z_send, z_near, (along(d, 1), v, p)).start()
    for level in range(2):
        past = STRIDE * (level + 1)
        for g in range(2):
            piece = pl.ds(g * GROUP, GROUP)
            for d in range(2):
                here = zbuf.at[slot(d, past), piece]
                arrived(here, z_pass.at[d, level, g])
                for more in (2, 1):
                    hops = past + more
                    if hops <= REACH[d][g]:
                        sem = z_near if hops == 3 else z_pass.at[d, 1, g] if hops == 4 else z_far
                        there = zbuf.at[slot(d, hops), piece]
                        remote(here, there, z_send, sem, (along(d, more), v, p)).start()

    arrived(gt.at[:3], g_recv)
    for step in (2, 4, 6):
        block = gt.at[lax.rem(v + step, NC)]
        remote(block, block, g_send, g_pass, (u, mate, p)).start()
    arrived(rows.at[:3], r_recv)
    for step in (2, 4, 6):
        block = rows.at[lax.rem(v + step, NC)]
        remote(block, block, r_send, r_pass, (u, mate, p)).start()
    arrived(gt.at[:4], g_pass)
    for r in range(NR):
        origin = along(r % 2, (r + 1) // 2)
        block = gt[:, pl.ds(pl.multiple_of(origin * BLOCK, BLOCK), BLOCK)]
        inverse[:, r * ROWS : (r + 1) * ROWS] = block.reshape(ROWS, ROWS).T
    arrived(rows.at[:4], r_pass)
    for a in range(NP):
        turned[a * LANES : (a + 1) * LANES] = rows[:, a].reshape(ROWS, LANES).T
    arrived(zbuf.at[:4], z_near)
    split = slot(0, 5)
    both = dot(inverse[:, : split * ROWS], zbuf[:split].reshape(split * ROWS, LANES))
    arrived(zbuf.at[:3], z_far)
    both = both + dot(inverse[:, split * ROWS :], zbuf[split:].reshape((NR - split) * ROWS, LANES))

    panel = ((swap_halves(both) - both) * weight).reshape(NC, BLOCK, LANES)
    panel_out[...] = pack(panel[:, : BLOCK // 2], panel[:, BLOCK // 2 :])
    both = both * weight
    for k in range(NP):
        a = lax.rem(v + NP // 2 + k, NP)
        out = dot(turned[pl.ds(pl.multiple_of(a * LANES, LANES), LANES)], both)
        terms[a] = out
        top = out[:CHUNK]
        qsend[a, :HALF] = jnp.where(low_lanes((HALF, LANES)), swap_halves(top[:HALF]), top[HALF:])
        qsend[a, HALF:] = panel_out[a]
        to_me = jnp.logical_and(v == p, a == v)

        @pl.when(to_me)
        def _():
            qrecv[p] = qsend[a]

        @pl.when(jnp.logical_not(to_me))
        def _():
            remote(qsend.at[a], qrecv.at[p], q_send, q_recv, (u, a, v)).start()

    for k in range(1, NP + 1):
        a = lax.rem(p + k, NP)
        out = terms[a]
        top, bottom = out[:CHUNK], out[CHUNK:]
        own_part = fixed[pl.ds(pl.multiple_of(a * CHUNK, CHUNK), CHUNK)]
        first = (top - swap_halves(top)) + swap_halves(bottom) + own_part
        packed = pack(first[:HALF], first[HALF:])
        if k == NP:
            frecv[p] = packed
        else:
            fsend[a] = packed
            remote(fsend.at[a], frecv.at[p], f_send, f_recv, (u, v, a)).start()

    arrived(frecv.at[: NP - 1], f_recv)

    @pl.when(v == p)
    def _():
        arrived(qrecv.at[: NP - 1], q_recv)

    @pl.when(v != p)
    def _():
        arrived(qrecv, q_recv)

    first, second = frecv[0], qrecv[0]
    for q in range(1, NP):
        first, second = first + frecv[q], second + qrecv[q]
    back = unpack(second[:HALF])
    back = jnp.concatenate([back, back], axis=0).T[:CHUNK]
    total = unpack(first) - back
    tsend[...] = pack(total[:HALF], total[HALF:])
    for step in FAR_FIRST:
        to = lax.rem(u + step, NR)
        remote(tsend, trecv.at[u], t_send, t_recv, (to, v, p)).start()
    trecv[u] = tsend[...]
    panel_ref[...] = unpack(second[HALF:])[:, :CHUNK]

    arrived(trecv.at[: NR - 1], t_recv)
    total = trecv[0]
    for k in range(1, NR):
        total = total + trecv[k]
    diag_ref[...] = unpack(total)[:, :CHUNK]

    left(own.at[: NC - 1], tile_send)
    left(gt.at[: NC - 1], g_send)
    left(rows.at[: NC - 1], r_send)
    left(zbuf.at[: NR - 1], z_send)
    left(fsend.at[: NP - 1], f_send)
    left(trecv.at[: NR - 1], t_send)

    @pl.when(v == p)
    def _():
        left(qsend.at[: NP - 1], q_send)

    @pl.when(v != p)
    def _():
        left(qsend, q_send)


def shards(
    inverse_grid, factor_b, factor_a, coupling_a, diag_inv_b, diag_inv_a, pole_weights, structure
):
    hbm = pl.BlockSpec(memory_space=pltpu.HBM)
    vmem = pl.BlockSpec(memory_space=pltpu.VMEM)
    dma = pltpu.SemaphoreType.DMA
    panel, diag = pl.pallas_call(
        kernel,
        out_shape=(
            pltpu.VMEM((BLOCK, CHUNK), F32),
            pltpu.VMEM((CHUNK, CHUNK), F32),
        ),
        in_specs=[hbm] * 8,
        out_specs=(vmem, vmem),
        scratch_shapes=[
            pltpu.SMEM((1,), F32),
            pltpu.SMEM((2,), jnp.int32),
            pltpu.VMEM((NC, NR * BLOCK, ROWS), F32),
            pltpu.VMEM((BLOCK, WIDTH), F32),
            pltpu.VMEM((BLOCK, WIDTH), F32),
            pltpu.VMEM((WIDTH, WIDTH), F32),
            pltpu.VMEM((CHUNK, WIDTH), F32),
            pltpu.VMEM((CHUNK, LANES), F32),
            pltpu.VMEM((WIDTH, LANES), F32),
            pltpu.VMEM((NC, BLOCK, LANES), F32),
            pltpu.VMEM((NR, NC, BLOCK, LANES), F32),
            pltpu.VMEM((NC, NC, BLOCK, LANES), F32),
            pltpu.VMEM((ROWS, NR * ROWS), F32),
            pltpu.VMEM((NP * LANES, ROWS), F32),
            pltpu.VMEM((NP, LANES, LANES), F32),
            pltpu.VMEM((NC, BLOCK // 2, LANES), F32),
            pltpu.VMEM((NP, HALF, LANES), F32),
            pltpu.VMEM((NP, HALF, LANES), F32),
            pltpu.VMEM((NP, HALF + BLOCK // 2, LANES), F32),
            pltpu.VMEM((NP, HALF + BLOCK // 2, LANES), F32),
            pltpu.VMEM((HALF, LANES), F32),
            pltpu.VMEM((NR, HALF, LANES), F32),
            dma((5,)), dma((3,)), dma, dma, dma, dma, dma, dma, dma((2, 2, 2)), dma, dma,
            dma, dma, dma, dma, dma, dma, dma, dma, dma,
        ],
        compiler_params=pltpu.CompilerParams(collective_id=0, has_side_effects=True),
    )(
        inverse_grid[0, 0, :, 0, :].T,
        factor_b[0, 0, 0],
        factor_a[0, 0, 0],
        coupling_a[0],
        diag_inv_b[0],
        diag_inv_a[0],
        pole_weights,
        structure[:, 0, 0],
    )
    return panel[None, None], diag


def solution(mesh):
    in_specs = (
        P("poles", "rows", None, "cols", None),
        P("poles", "rows", "cols", None, None),
        P("poles", "rows", "cols", None, None),
        P("poles", None, None),
        P("poles", None, None),
        P("poles", None, None),
        P("poles"),
        P(None, "rows", "cols"),
    )
    out_specs = (P("rows", "cols", None, "poles"), P("poles", "cols"))
    return jax.shard_map(shards, mesh=mesh, in_specs=in_specs, out_specs=out_specs, check_vma=False)
```

```python
import jax
import jax.numpy as jnp
from jax import lax
from jax.experimental import pallas as pl
from jax.experimental.pallas import tpu as pltpu
from jax.sharding import PartitionSpec as P

MESH = pl.DeviceIdType.MESH
F32 = jnp.float32
WIDTH, BLOCK = 512, 16
NR, NC, NP = 12, 8, 8
CHUNK = WIDTH // NP
LANES = 2 * CHUNK
ROWS = NC * BLOCK
HALF = CHUNK // 2
STRIDE = 2
REACH = ((6, 5), (5, 6))
CHIPS = NC // 2
NEAREST = (0, 1, 3, 2)
FAR_FIRST = sorted(range(1, NR), key=lambda step: -min(step, NR - step))
REACH = ((6, 5), (5, 6))


def dot(left, right, contract=((1,), (0,))):
    return lax.dot_general(
        left, right, (contract, ((), ())), precision=lax.Precision.HIGH, preferred_element_type=F32
    )


def halves(x):
    high = x.astype(jnp.bfloat16)
    return high, (x - high.astype(F32)).astype(jnp.bfloat16)


def swap_halves(x):
    return pltpu.roll(x, CHUNK, axis=x.ndim - 1)


def low_lanes(shape):
    return lax.broadcasted_iota(jnp.int32, shape, len(shape) - 1) < CHUNK


def pack(top, bottom):
    return jnp.where(low_lanes(top.shape), top, swap_halves(bottom))


def unpack(x):
    return jnp.concatenate([x, swap_halves(x)], axis=0)


def remote(src, dst, send, recv, to):
    return pltpu.make_async_remote_copy(
        src_ref=src, dst_ref=dst, send_sem=send, recv_sem=recv, device_id=to, device_id_type=MESH
    )


def kernel(
    g_hbm, lb_hbm, la_hbm, c_hbm, db_hbm, da_hbm, weight_hbm, keep_hbm,
    panel_ref, diag_ref,
    weight_s, keep_s, gt, lb, la, coup, dbk, dak, fixed, own, zbuf, rows, inverse, turned, terms, panel_out,
    fsend, frecv, qsend, qrecv, tsend, trecv,
    load_sem, late_sem, tile_send, tile_recv, g_send, g_recv, g_opp, g_pass, z_send, z_pass, z_near, z_far, z_last,
    r_send, r_recv, r_opp, r_pass, f_send, f_recv, q_send, q_recv, t_send, t_recv,
):
    u, v, p = lax.axis_index("rows"), lax.axis_index("cols"), lax.axis_index("poles")
    h, chip = lax.rem(v, 2), v // 2
    mate = chip * 2 + 1 - h
    part = jnp.minimum(u, NP - 1)

    lanes = pl.ds(pl.multiple_of(chip * LANES, LANES), LANES)
    loads = [
        pltpu.make_async_copy(lb_hbm, lb, load_sem.at[0]),
        pltpu.make_async_copy(la_hbm, la, load_sem.at[1]),
        pltpu.make_async_copy(c_hbm, coup, load_sem.at[2]),
        pltpu.make_async_copy(weight_hbm, weight_s, load_sem.at[3]),
        pltpu.make_async_copy(keep_hbm, keep_s, load_sem.at[4]),
    ]
    later = [
        pltpu.make_async_copy(g_hbm, gt.at[v], late_sem.at[0]),
        pltpu.make_async_copy(db_hbm.at[pl.ds(part * CHUNK, CHUNK)], dbk, late_sem.at[1]),
        pltpu.make_async_copy(da_hbm.at[pl.ds(part * CHUNK, CHUNK), lanes], dak, late_sem.at[2]),
    ]
    for copy in loads + later:
        copy.start()

    barrier = pltpu.get_barrier_semaphore()

    def greet(to):
        pl.semaphore_signal(barrier, inc=1, device_id=to, device_id_type=MESH)

    for step in range(1, STRIDE + 1):
        greet((lax.rem(u + step, NR), v, p))
        greet((lax.rem(u + NR - step, NR), v, p))
    for step in range(1, NC):
        greet((u, lax.rem(v + step, NC), p))
        greet((u, v, lax.rem(p + step, NP)))

    for copy in loads:
        copy.wait()
    weight = weight_s[0]
    keep_b = keep_s[0].astype(F32)
    keep_a = keep_s[1].astype(F32)
    panel_a = la[...] * keep_a
    panel_n = dot(lb[...] * keep_b, coup[...])
    for pair in range(NC // 2):
        a, n = (x[:, pair * LANES : (pair + 1) * LANES] for x in (panel_a, panel_n))
        own[2 * pair] = pack(a, n)
        own[2 * pair + 1] = jnp.where(low_lanes(a.shape), swap_halves(a), n)
    pl.semaphore_wait(barrier, 2 * STRIDE + (NC - 1) + (NP - 1))

    def along(d, hops):
        return lax.rem(u + (hops if d == 0 else NR - hops), NR)

    def slot(d, hops):
        return min(2 * hops - 1 + d, NR - 1)

    def arrived(buf, sem):
        remote(buf, buf, tile_send, sem, (u, mate, p)).wait_recv()

    def left(buf, sem):
        remote(buf, buf, sem, g_recv, (u, mate, p)).wait_send()

    for step in (1, 2, 6, 3, 7, 4, 5):
        to = lax.rem(v + step, NC)
        back = tile_recv.at[lax.rem(chip + CHIPS - to // 2, CHIPS)]
        remote(own.at[to], zbuf.at[0, v], tile_send, back, (u, to, p)).start()
    zbuf[0, v] = own[v]
    rows[v] = own[...]
    later[0].wait()
    for step in (2, 6):
        remote(gt.at[v], gt.at[v], g_send, g_recv, (u, lax.rem(v + step, NC), p)).start()
    remote(gt.at[v], gt.at[v], g_send, g_pass, (u, mate, p)).start()
    for step in (2, 6):
        remote(own, rows.at[v], r_send, r_recv, (u, lax.rem(v + step, NC), p)).start()
    remote(own, rows.at[v], r_send, r_pass, (u, mate, p)).start()

    def tiles(k):
        return pl.ds(2 * lax.rem(chip + k, CHIPS), 2)

    for k in NEAREST:
        arrived(zbuf.at[0, : 2 if k else 1], tile_recv.at[k])
        for hops in (STRIDE, 1):
            for d in range(2):
                sem = z_near if hops == 1 else z_pass.at[d, 0, k]
                to = (along(d, hops), v, p)
                remote(zbuf.at[0, tiles(k)], zbuf.at[slot(d, hops), tiles(k)], z_send, sem, to).start()

    for copy in later[1:]:
        copy.wait()
    scale = weight * (u < NP).astype(F32)
    inner = dot(dbk[...], coup[:, lanes])
    inner = jnp.where(h == 0, inner, swap_halves(inner)) * scale
    fixed[...] = dot(coup[pl.ds(part * CHUNK, CHUNK), :], inner, ((0,), (0,)))
    block = jnp.where(h == 0, dak[...], swap_halves(dak[...])) * scale
    fixed[pl.ds(part * CHUNK, CHUNK)] += block

    def relay(level):
        past = STRIDE * (level + 1)
        for k in NEAREST:
            for d in range(2):
                here = zbuf.at[slot(d, past), tiles(k)]
                arrived(here, z_pass.at[d, level, k])
                for more in (2, 1):
                    hops = past + more
                    if hops <= REACH[d][k % 2]:
                        sem = z_near if hops == 3 else z_pass.at[d, 1, k] if hops == 4 else z_far if hops == 5 else z_last
                        there = zbuf.at[slot(d, hops), tiles(k)]
                        remote(here, there, z_send, sem, (along(d, more), v, p)).start()

    def across(buf, send, recv, onward, final):
        arrived(buf.at[:2], recv)
        size = buf.shape[1] // 2
        for half, (source, to) in enumerate(((6, 2), (2, 6))):
            source = lax.rem(v + source, NC)
            block = buf.at[source, pl.ds(half * size, size)]
            remote(block, block, send, onward, (u, lax.rem(v + to, NC), p)).start()
            remote(buf.at[source], buf.at[source], send, final, (u, mate, p)).start()

    def opposite(buf, send, onward, final):
        block = buf.at[lax.rem(v + 4, NC)]
        arrived(block, onward)
        remote(block, block, send, final, (u, mate, p)).start()

    relay(0)
    across(gt, g_send, g_recv, g_opp, g_pass)
    across(rows, r_send, r_recv, r_opp, r_pass)
    relay(1)

    opposite(gt, g_send, g_opp, g_pass)
    opposite(rows, r_send, r_opp, r_pass)
    arrived(gt.at[:4], g_pass)
    for r in range(NR):
        origin = along(r % 2, (r + 1) // 2)
        block = gt[:, pl.ds(pl.multiple_of(origin * BLOCK, BLOCK), BLOCK)]
        inverse[:, r * ROWS : (r + 1) * ROWS] = block.reshape(ROWS, ROWS).T
    arrived(rows.at[:4], r_pass)
    for a in range(NP):
        high, low = halves(rows[:, a].reshape(ROWS, LANES).T)
        turned[a * LANES : (a + 1) * LANES, :ROWS] = high
        turned[a * LANES : (a + 1) * LANES, ROWS:] = low
    arrived(zbuf.at[:4], z_near)
    split, last = slot(0, 5), slot(0, 6)
    both = dot(inverse[:, : split * ROWS], zbuf[:split].reshape(split * ROWS, LANES))
    arrived(zbuf.at[:2], z_far)
    both = both + dot(inverse[:, split * ROWS : last * ROWS], zbuf[split:last].reshape(2 * ROWS, LANES))
    arrived(zbuf.at[0], z_last)
    both = both + dot(inverse[:, last * ROWS :], zbuf[last].reshape(ROWS, LANES))

    panel = ((swap_halves(both) - both) * weight).reshape(NC, BLOCK, LANES)
    panel_out[...] = pack(panel[:, : BLOCK // 2], panel[:, BLOCK // 2 :])
    high, low = halves(both * weight)
    right = jnp.concatenate([high, low], axis=1)
    right = jnp.concatenate([right, jnp.concatenate([high, jnp.zeros_like(low)], axis=1)], axis=0)
    out = lax.dot_general(turned[...], right, (((1,), (0,)), ((), ())), preferred_element_type=F32)
    terms[...] = (out[:, :LANES] + out[:, LANES:]).reshape(NP, LANES, LANES)
    for k in range(NP):
        a = lax.rem(v + NP // 2 + k, NP)
        top = terms[a, :CHUNK]
        qsend[a, :HALF] = jnp.where(low_lanes((HALF, LANES)), swap_halves(top[:HALF]), top[HALF:])
        qsend[a, HALF:] = panel_out[a]
        to_me = jnp.logical_and(v == p, a == v)

        @pl.when(to_me)
        def _():
            qrecv[p] = qsend[a]

        @pl.when(jnp.logical_not(to_me))
        def _():
            remote(qsend.at[a], qrecv.at[p], q_send, q_recv, (u, a, v)).start()

    for k in range(1, NP + 1):
        a = lax.rem(p + k, NP)
        out = terms[a]
        top, bottom = out[:CHUNK], out[CHUNK:]
        own_part = fixed[pl.ds(pl.multiple_of(a * CHUNK, CHUNK), CHUNK)]
        first = (top - swap_halves(top)) + swap_halves(bottom) + own_part
        packed = pack(first[:HALF], first[HALF:])
        if k == NP:
            frecv[p] = packed
        else:
            fsend[a] = packed
            remote(fsend.at[a], frecv.at[p], f_send, f_recv, (u, v, a)).start()

    arrived(frecv.at[: NP - 1], f_recv)

    @pl.when(v == p)
    def _():
        arrived(qrecv.at[: NP - 1], q_recv)

    @pl.when(v != p)
    def _():
        arrived(qrecv, q_recv)

    first, second = frecv[0], qrecv[0]
    for q in range(1, NP):
        first, second = first + frecv[q], second + qrecv[q]
    back = unpack(second[:HALF])
    back = jnp.concatenate([back, back], axis=0).T[:CHUNK]
    total = unpack(first) - back
    tsend[...] = pack(total[:HALF], total[HALF:])
    for step in FAR_FIRST:
        to = lax.rem(u + step, NR)
        remote(tsend, trecv.at[u], t_send, t_recv, (to, v, p)).start()
    trecv[u] = tsend[...]
    panel_ref[...] = unpack(second[HALF:])[:, :CHUNK]

    arrived(trecv.at[: NR - 1], t_recv)
    total = trecv[0]
    for k in range(1, NR):
        total = total + trecv[k]
    diag_ref[...] = unpack(total)[:, :CHUNK]

    left(own.at[: NC - 1], tile_send)
    left(gt.at[: NC - 1], g_send)
    left(rows.at[: NC - 1], r_send)
    left(zbuf.at[: NR - 1], z_send)
    left(fsend.at[: NP - 1], f_send)
    left(trecv.at[: NR - 1], t_send)

    @pl.when(v == p)
    def _():
        left(qsend.at[: NP - 1], q_send)

    @pl.when(v != p)
    def _():
        left(qsend, q_send)


def shards(
    inverse_grid, factor_b, factor_a, coupling_a, diag_inv_b, diag_inv_a, pole_weights, structure
):
    hbm = pl.BlockSpec(memory_space=pltpu.HBM)
    vmem = pl.BlockSpec(memory_space=pltpu.VMEM)
    dma = pltpu.SemaphoreType.DMA
    panel, diag = pl.pallas_call(
        kernel,
        out_shape=(
            pltpu.VMEM((BLOCK, CHUNK), F32),
            pltpu.VMEM((CHUNK, CHUNK), F32),
        ),
        in_specs=[hbm] * 8,
        out_specs=(vmem, vmem),
        scratch_shapes=[
            pltpu.SMEM((1,), F32),
            pltpu.SMEM((2,), jnp.int32),
            pltpu.VMEM((NC, NR * BLOCK, ROWS), F32),
            pltpu.VMEM((BLOCK, WIDTH), F32),
            pltpu.VMEM((BLOCK, WIDTH), F32),
            pltpu.VMEM((WIDTH, WIDTH), F32),
            pltpu.VMEM((CHUNK, WIDTH), F32),
            pltpu.VMEM((CHUNK, LANES), F32),
            pltpu.VMEM((WIDTH, LANES), F32),
            pltpu.VMEM((NC, BLOCK, LANES), F32),
            pltpu.VMEM((NR, NC, BLOCK, LANES), F32),
            pltpu.VMEM((NC, NC, BLOCK, LANES), F32),
            pltpu.VMEM((ROWS, NR * ROWS), F32),
            pltpu.VMEM((NP * LANES, 2 * ROWS), jnp.bfloat16),
            pltpu.VMEM((NP, LANES, LANES), F32),
            pltpu.VMEM((NC, BLOCK // 2, LANES), F32),
            pltpu.VMEM((NP, HALF, LANES), F32),
            pltpu.VMEM((NP, HALF, LANES), F32),
            pltpu.VMEM((NP, HALF + BLOCK // 2, LANES), F32),
            pltpu.VMEM((NP, HALF + BLOCK // 2, LANES), F32),
            pltpu.VMEM((HALF, LANES), F32),
            pltpu.VMEM((NR, HALF, LANES), F32),
            dma((5,)), dma((3,)), dma, dma((NC // 2,)), dma, dma, dma, dma, dma, dma((2, 2, NC // 2)), dma, dma, dma, dma,
            dma, dma, dma, dma, dma, dma, dma, dma, dma,
        ],
        compiler_params=pltpu.CompilerParams(collective_id=0, has_side_effects=True),
    )(
        inverse_grid[0, 0, :, 0, :].T,
        factor_b[0, 0, 0],
        factor_a[0, 0, 0],
        coupling_a[0],
        diag_inv_b[0],
        diag_inv_a[0],
        pole_weights,
        structure[:, 0, 0],
    )
    return panel[None, None], diag


def solution(mesh):
    in_specs = (
        P("poles", "rows", None, "cols", None),
        P("poles", "rows", "cols", None, None),
        P("poles", "rows", "cols", None, None),
        P("poles", None, None),
        P("poles", None, None),
        P("poles", None, None),
        P("poles"),
        P(None, "rows", "cols"),
    )
    out_specs = (P("rows", "cols", None, "poles"), P("poles", "cols"))
    return jax.shard_map(shards, mesh=mesh, in_specs=in_specs, out_specs=out_specs, check_vma=False)
```

```python
import jax
import jax.numpy as jnp
from jax import lax
from jax.experimental import pallas as pl
from jax.experimental.pallas import tpu as pltpu
from jax.sharding import PartitionSpec as P

MESH = pl.DeviceIdType.MESH
F32 = jnp.float32
WIDTH, BLOCK = 512, 16
NR, NC, NP = 12, 8, 8
CHUNK = WIDTH // NP
LANES = 2 * CHUNK
ROWS = NC * BLOCK
HALF = CHUNK // 2
STRIDE = 2
REACH = ((6, 5), (5, 6))
CHIPS = NC // 2
NEAREST = (0, 1, 3, 2)
FAR_FIRST = sorted(range(1, NR), key=lambda step: -min(step, NR - step))
REACH = ((6, 5), (5, 6))


def dot(left, right, contract=((1,), (0,))):
    return lax.dot_general(
        left, right, (contract, ((), ())), precision=lax.Precision.HIGH, preferred_element_type=F32
    )


def halves(x):
    high = x.astype(jnp.bfloat16)
    return high, (x - high.astype(F32)).astype(jnp.bfloat16)


def swap_halves(x):
    return pltpu.roll(x, CHUNK, axis=x.ndim - 1)


def low_lanes(shape):
    return lax.broadcasted_iota(jnp.int32, shape, len(shape) - 1) < CHUNK


def pack(top, bottom):
    return jnp.where(low_lanes(top.shape), top, swap_halves(bottom))


def unpack(x):
    return jnp.concatenate([x, swap_halves(x)], axis=0)


def remote(src, dst, send, recv, to):
    return pltpu.make_async_remote_copy(
        src_ref=src, dst_ref=dst, send_sem=send, recv_sem=recv, device_id=to, device_id_type=MESH
    )


def kernel(
    g_hbm, lb_hbm, la_hbm, c_hbm, db_hbm, da_hbm, weight_hbm, keep_hbm,
    panel_ref, diag_ref,
    weight_s, keep_s, gt, lb, la, coup, dbk, dak, fixed, own, zbuf, rows, inverse, turned, terms, panel_out,
    fsend, frecv, qsend, qrecv, tsend, trecv,
    load_sem, late_sem, tile_send, tile_recv, g_send, g_recv, g_opp, g_pass, z_send, z_pass, z_rest, g_last,
    r_send, r_recv, r_opp, r_pass, f_send, f_recv, q_send, q_recv, t_send, t_recv,
):
    u, v, p = lax.axis_index("rows"), lax.axis_index("cols"), lax.axis_index("poles")
    h, chip = lax.rem(v, 2), v // 2
    mate = chip * 2 + 1 - h
    part = jnp.minimum(u, NP - 1)

    lanes = pl.ds(pl.multiple_of(chip * LANES, LANES), LANES)
    loads = [
        pltpu.make_async_copy(lb_hbm, lb, load_sem.at[0]),
        pltpu.make_async_copy(la_hbm, la, load_sem.at[1]),
        pltpu.make_async_copy(c_hbm, coup, load_sem.at[2]),
        pltpu.make_async_copy(weight_hbm, weight_s, load_sem.at[3]),
        pltpu.make_async_copy(keep_hbm, keep_s, load_sem.at[4]),
    ]
    later = [
        pltpu.make_async_copy(g_hbm, gt.at[v], late_sem.at[0]),
        pltpu.make_async_copy(db_hbm.at[pl.ds(part * CHUNK, CHUNK)], dbk, late_sem.at[1]),
        pltpu.make_async_copy(da_hbm.at[pl.ds(part * CHUNK, CHUNK), lanes], dak, late_sem.at[2]),
    ]
    for copy in loads + later:
        copy.start()

    barrier = pltpu.get_barrier_semaphore()

    def greet(to):
        pl.semaphore_signal(barrier, inc=1, device_id=to, device_id_type=MESH)

    for step in (4, 5, 3, 2, 6, 7, 1):
        greet((u, lax.rem(v + step, NC), p))
    for step in range(1, NP):
        greet((u, v, lax.rem(p + step, NP)))
    for step in range(1, STRIDE + 1):
        greet((lax.rem(u + step, NR), v, p))
        greet((lax.rem(u + NR - step, NR), v, p))

    for copy in loads:
        copy.wait()
    weight = weight_s[0]
    keep_b = keep_s[0].astype(F32)
    keep_a = keep_s[1].astype(F32)
    panel_a = la[...] * keep_a
    panel_n = dot(lb[...] * keep_b, coup[...])
    for pair in range(NC // 2):
        a, n = (x[:, pair * LANES : (pair + 1) * LANES] for x in (panel_a, panel_n))
        own[2 * pair] = pack(a, n)
        own[2 * pair + 1] = jnp.where(low_lanes(a.shape), swap_halves(a), n)
    pl.semaphore_wait(barrier, 2 * STRIDE + (NC - 1) + (NP - 1))

    def along(d, hops):
        return lax.rem(u + (hops if d == 0 else NR - hops), NR)

    def slot(d, hops):
        return min(2 * hops - 1 + d, NR - 1)

    def arrived(buf, sem):
        remote(buf, buf, tile_send, sem, (u, mate, p)).wait_recv()

    def left(buf, sem):
        remote(buf, buf, sem, g_recv, (u, mate, p)).wait_send()

    for step in (1, 2, 6, 3, 7, 4, 5):
        to = lax.rem(v + step, NC)
        back = tile_recv.at[lax.rem(chip + CHIPS - to // 2, CHIPS)]
        remote(own.at[to], zbuf.at[0, v], tile_send, back, (u, to, p)).start()
    zbuf[0, v] = own[v]
    rows[v] = own[...]
    later[0].wait()
    for step in (2, 6):
        remote(gt.at[v], gt.at[v], g_send, g_recv, (u, lax.rem(v + step, NC), p)).start()
    remote(gt.at[v], gt.at[v], g_send, g_pass, (u, mate, p)).start()
    for step in (2, 6):
        remote(own, rows.at[v], r_send, r_recv, (u, lax.rem(v + step, NC), p)).start()
    remote(own, rows.at[v], r_send, r_pass, (u, mate, p)).start()

    def tiles(k):
        return pl.ds(2 * lax.rem(chip + k, CHIPS), 2)

    for k in NEAREST:
        arrived(zbuf.at[0, : 2 if k else 1], tile_recv.at[k])
        for hops in (STRIDE, 1):
            for d in range(2):
                sem = z_rest.at[k] if hops == 1 else z_pass.at[d, 0, k]
                to = (along(d, hops), v, p)
                remote(zbuf.at[0, tiles(k)], zbuf.at[slot(d, hops), tiles(k)], z_send, sem, to).start()

    for copy in later[1:]:
        copy.wait()
    scale = weight * (u < NP).astype(F32)
    inner = dot(dbk[...], coup[:, lanes])
    inner = jnp.where(h == 0, inner, swap_halves(inner)) * scale
    fixed[...] = dot(coup[pl.ds(part * CHUNK, CHUNK), :], inner, ((0,), (0,)))
    block = jnp.where(h == 0, dak[...], swap_halves(dak[...])) * scale
    fixed[pl.ds(part * CHUNK, CHUNK)] += block

    def relay(level):
        past = STRIDE * (level + 1)
        for k in NEAREST:
            for d in range(2):
                here = zbuf.at[slot(d, past), tiles(k)]
                arrived(here, z_pass.at[d, level, k])
                for more in (2, 1):
                    hops = past + more
                    if hops <= REACH[d][k % 2]:
                        sem = z_pass.at[d, 1, k] if hops == 4 else z_rest.at[k]
                        there = zbuf.at[slot(d, hops), tiles(k)]
                        remote(here, there, z_send, sem, (along(d, more), v, p)).start()

    def across(buf, send, recv, onward, final):
        arrived(buf.at[:2], recv)
        size = buf.shape[1] // 2
        for half, (source, to) in enumerate(((6, 2), (2, 6))):
            source = lax.rem(v + source, NC)
            block = buf.at[source, pl.ds(half * size, size)]
            remote(block, block, send, onward, (u, lax.rem(v + to, NC), p)).start()
            remote(buf.at[source], buf.at[source], send, final, (u, mate, p)).start()

    def opposite(buf, send, onward, final):
        block = buf.at[lax.rem(v + 4, NC)]
        arrived(block, onward)
        remote(block, block, send, final, (u, mate, p)).start()

    relay(0)
    across(gt, g_send, g_recv, g_opp, g_pass)
    across(rows, r_send, r_recv, r_opp, r_pass)
    relay(1)

    def share(k):
        parts = []
        for r in range(NR):
            origin = along(r % 2, (r + 1) // 2)
            at = pl.ds(pl.multiple_of(origin * BLOCK, BLOCK), BLOCK)
            parts.append(gt[tiles(k), at].reshape(2 * BLOCK, ROWS))
        inverse[k] = jnp.concatenate(parts, axis=0).T

    def column_sum(k):
        arrived(zbuf.at[: NR // 2 + 1, :2], z_rest.at[k])
        return dot(inverse[k], zbuf[:, tiles(k)].reshape(2 * NR * BLOCK, LANES))

    arrived(gt.at[:3], g_pass)
    for k in NEAREST[:3]:
        share(k)
    opposite(gt, g_send, g_opp, g_last)
    opposite(rows, r_send, r_opp, r_pass)
    both = column_sum(NEAREST[0])
    for k in NEAREST[1:3]:
        both = both + column_sum(k)
    arrived(gt.at[0], g_last)
    share(NEAREST[3])
    both = both + column_sum(NEAREST[3])
    arrived(rows.at[:4], r_pass)
    for a in range(NP):
        high, low = halves(rows[:, a].reshape(ROWS, LANES).T)
        turned[a * LANES : (a + 1) * LANES, :ROWS] = high
        turned[a * LANES : (a + 1) * LANES, ROWS:] = low

    panel = ((swap_halves(both) - both) * weight).reshape(NC, BLOCK, LANES)
    panel_out[...] = pack(panel[:, : BLOCK // 2], panel[:, BLOCK // 2 :])
    high, low = halves(both * weight)
    right = jnp.concatenate([high, low], axis=1)
    right = jnp.concatenate([right, jnp.concatenate([high, jnp.zeros_like(low)], axis=1)], axis=0)
    half = NP // 2
    for part in range(2):
        begin = half * lax.rem(v // half + 1 + part, 2)
        lhs = turned[pl.ds(pl.multiple_of(begin * LANES, half * LANES), half * LANES)]
        out = lax.dot_general(lhs, right, (((1,), (0,)), ((), ())), preferred_element_type=F32)
        out = (out[:, :LANES] + out[:, LANES:]).reshape(half, LANES, LANES)
        terms[pl.ds(begin, half)] = out
        for k in range(half):
            a, top = begin + k, out[k, :CHUNK]
            qsend[a, :HALF] = jnp.where(low_lanes((HALF, LANES)), swap_halves(top[:HALF]), top[HALF:])
            qsend[a, HALF:] = panel_out[a]
            to_me = jnp.logical_and(v == p, a == v)

            @pl.when(to_me)
            def _():
                qrecv[p] = qsend[a]

            @pl.when(jnp.logical_not(to_me))
            def _():
                remote(qsend.at[a], qrecv.at[p], q_send, q_recv, (u, a, v)).start()

    for k in range(1, NP + 1):
        a = lax.rem(p + k, NP)
        out = terms[a]
        top, bottom = out[:CHUNK], out[CHUNK:]
        own_part = fixed[pl.ds(pl.multiple_of(a * CHUNK, CHUNK), CHUNK)]
        first = (top - swap_halves(top)) + swap_halves(bottom) + own_part
        packed = pack(first[:HALF], first[HALF:])
        if k == NP:
            frecv[p] = packed
        else:
            fsend[a] = packed
            remote(fsend.at[a], frecv.at[p], f_send, f_recv, (u, v, a)).start()

    arrived(frecv.at[: NP - 1], f_recv)

    @pl.when(v == p)
    def _():
        arrived(qrecv.at[: NP - 1], q_recv)

    @pl.when(v != p)
    def _():
        arrived(qrecv, q_recv)

    first, second = frecv[0], qrecv[0]
    for q in range(1, NP):
        first, second = first + frecv[q], second + qrecv[q]
    back = unpack(second[:HALF])
    back = jnp.concatenate([back, back], axis=0).T[:CHUNK]
    total = unpack(first) - back
    tsend[...] = pack(total[:HALF], total[HALF:])
    for step in FAR_FIRST:
        to = lax.rem(u + step, NR)
        remote(tsend, trecv.at[u], t_send, t_recv, (to, v, p)).start()
    trecv[u] = tsend[...]
    panel_ref[...] = unpack(second[HALF:])[:, :CHUNK]

    arrived(trecv.at[: NR - 1], t_recv)
    total = trecv[0]
    for k in range(1, NR):
        total = total + trecv[k]
    diag_ref[...] = unpack(total)[:, :CHUNK]

    left(own.at[: NC - 1], tile_send)
    left(gt.at[: NC - 1], g_send)
    left(rows.at[: NC - 1], r_send)
    left(zbuf.at[: NR - 1], z_send)
    left(fsend.at[: NP - 1], f_send)
    left(trecv.at[: NR - 1], t_send)

    @pl.when(v == p)
    def _():
        left(qsend.at[: NP - 1], q_send)

    @pl.when(v != p)
    def _():
        left(qsend, q_send)


def shards(
    inverse_grid, factor_b, factor_a, coupling_a, diag_inv_b, diag_inv_a, pole_weights, structure
):
    hbm = pl.BlockSpec(memory_space=pltpu.HBM)
    vmem = pl.BlockSpec(memory_space=pltpu.VMEM)
    dma = pltpu.SemaphoreType.DMA
    panel, diag = pl.pallas_call(
        kernel,
        out_shape=(
            pltpu.VMEM((BLOCK, CHUNK), F32),
            pltpu.VMEM((CHUNK, CHUNK), F32),
        ),
        in_specs=[hbm] * 8,
        out_specs=(vmem, vmem),
        scratch_shapes=[
            pltpu.SMEM((1,), F32),
            pltpu.SMEM((2,), jnp.int32),
            pltpu.VMEM((NC, NR * BLOCK, ROWS), F32),
            pltpu.VMEM((BLOCK, WIDTH), F32),
            pltpu.VMEM((BLOCK, WIDTH), F32),
            pltpu.VMEM((WIDTH, WIDTH), F32),
            pltpu.VMEM((CHUNK, WIDTH), F32),
            pltpu.VMEM((CHUNK, LANES), F32),
            pltpu.VMEM((WIDTH, LANES), F32),
            pltpu.VMEM((NC, BLOCK, LANES), F32),
            pltpu.VMEM((NR, NC, BLOCK, LANES), F32),
            pltpu.VMEM((NC, NC, BLOCK, LANES), F32),
            pltpu.VMEM((CHIPS, ROWS, 2 * NR * BLOCK), F32),
            pltpu.VMEM((NP * LANES, 2 * ROWS), jnp.bfloat16),
            pltpu.VMEM((NP, LANES, LANES), F32),
            pltpu.VMEM((NC, BLOCK // 2, LANES), F32),
            pltpu.VMEM((NP, HALF, LANES), F32),
            pltpu.VMEM((NP, HALF, LANES), F32),
            pltpu.VMEM((NP, HALF + BLOCK // 2, LANES), F32),
            pltpu.VMEM((NP, HALF + BLOCK // 2, LANES), F32),
            pltpu.VMEM((HALF, LANES), F32),
            pltpu.VMEM((NR, HALF, LANES), F32),
            dma((5,)), dma((3,)), dma, dma((NC // 2,)), dma, dma, dma, dma, dma, dma((2, 2, NC // 2)), dma((NC // 2,)), dma, dma,
            dma, dma, dma, dma, dma, dma, dma, dma, dma,
        ],
        compiler_params=pltpu.CompilerParams(collective_id=0, has_side_effects=True),
    )(
        inverse_grid[0, 0, :, 0, :].T,
        factor_b[0, 0, 0],
        factor_a[0, 0, 0],
        coupling_a[0],
        diag_inv_b[0],
        diag_inv_a[0],
        pole_weights,
        structure[:, 0, 0],
    )
    return panel[None, None], diag


def solution(mesh):
    in_specs = (
        P("poles", "rows", None, "cols", None),
        P("poles", "rows", "cols", None, None),
        P("poles", "rows", "cols", None, None),
        P("poles", None, None),
        P("poles", None, None),
        P("poles", None, None),
        P("poles"),
        P(None, "rows", "cols"),
    )
    out_specs = (P("rows", "cols", None, "poles"), P("poles", "cols"))
    return jax.shard_map(shards, mesh=mesh, in_specs=in_specs, out_specs=out_specs, check_vma=False)
```

```python
import jax
import jax.numpy as jnp
from jax import lax
from jax.experimental import pallas as pl
from jax.experimental.pallas import tpu as pltpu
from jax.sharding import PartitionSpec as P

MESH = pl.DeviceIdType.MESH
F32 = jnp.float32
WIDTH, BLOCK = 512, 16
NR, NC, NP = 12, 8, 8
CHUNK = WIDTH // NP
LANES = 2 * CHUNK
ROWS = NC * BLOCK
HALF = CHUNK // 2
STRIDE = 2
REACH = ((6, 5), (5, 6))
CHIPS = NC // 2
NEAREST = (0, 1, 3, 2)
FAR_FIRST = sorted(range(1, NR), key=lambda step: -min(step, NR - step))
REACH = ((6, 5), (5, 6))


def dot(left, right, contract=((1,), (0,))):
    return lax.dot_general(
        left, right, (contract, ((), ())), precision=lax.Precision.HIGH, preferred_element_type=F32
    )


def halves(x):
    high = x.astype(jnp.bfloat16)
    return high, (x - high.astype(F32)).astype(jnp.bfloat16)


def swap_halves(x):
    return pltpu.roll(x, CHUNK, axis=x.ndim - 1)


def low_lanes(shape):
    return lax.broadcasted_iota(jnp.int32, shape, len(shape) - 1) < CHUNK


def pack(top, bottom):
    return jnp.where(low_lanes(top.shape), top, swap_halves(bottom))


def unpack(x):
    return jnp.concatenate([x, swap_halves(x)], axis=0)


def remote(src, dst, send, recv, to):
    return pltpu.make_async_remote_copy(
        src_ref=src, dst_ref=dst, send_sem=send, recv_sem=recv, device_id=to, device_id_type=MESH
    )


def kernel(
    g_hbm, lb_hbm, la_hbm, c_hbm, db_hbm, da_hbm, weight_hbm, keep_hbm,
    panel_ref, diag_ref,
    weight_s, keep_s, gt, lb, la, coup, dbk, dak, fixed, own, zbuf, rows, inverse, turned, panel_out, panel_in,
    fsend, frecv, qsend, qrecv, tsend, trecv,
    load_sem, late_sem, tile_send, tile_recv, g_send, g_recv, g_opp, g_pass, z_send, z_pass, z_rest, g_last,
    r_send, r_recv, r_opp, r_pass, f_send, f_recv, q_send, q_recv, t_send, t_recv, n_send, n_recv,
):
    u, v, p = lax.axis_index("rows"), lax.axis_index("cols"), lax.axis_index("poles")
    h, chip = lax.rem(v, 2), v // 2
    mate = chip * 2 + 1 - h
    part = jnp.minimum(u, NP - 1)

    lanes = pl.ds(pl.multiple_of(chip * LANES, LANES), LANES)
    loads = [
        pltpu.make_async_copy(lb_hbm, lb, load_sem.at[0]),
        pltpu.make_async_copy(la_hbm, la, load_sem.at[1]),
        pltpu.make_async_copy(c_hbm, coup, load_sem.at[2]),
        pltpu.make_async_copy(weight_hbm, weight_s, load_sem.at[3]),
        pltpu.make_async_copy(keep_hbm, keep_s, load_sem.at[4]),
    ]
    later = [
        pltpu.make_async_copy(g_hbm, gt.at[v], late_sem.at[0]),
        pltpu.make_async_copy(db_hbm.at[pl.ds(part * CHUNK, CHUNK)], dbk, late_sem.at[1]),
        pltpu.make_async_copy(da_hbm.at[pl.ds(part * CHUNK, CHUNK), lanes], dak, late_sem.at[2]),
    ]
    for copy in loads + later:
        copy.start()

    barrier = pltpu.get_barrier_semaphore()

    def greet(to):
        pl.semaphore_signal(barrier, inc=1, device_id=to, device_id_type=MESH)

    for step in (4, 5, 3, 2, 6, 7, 1):
        greet((u, lax.rem(v + step, NC), p))
    for step in range(1, NP):
        greet((u, v, lax.rem(p + step, NP)))
    for step in range(1, STRIDE + 1):
        greet((lax.rem(u + step, NR), v, p))
        greet((lax.rem(u + NR - step, NR), v, p))

    for copy in loads:
        copy.wait()
    weight = weight_s[0]
    keep_b = keep_s[0].astype(F32)
    keep_a = keep_s[1].astype(F32)
    panel_a = la[...] * keep_a
    panel_n = dot(lb[...] * keep_b, coup[...])
    for pair in range(NC // 2):
        a, n = (x[:, pair * LANES : (pair + 1) * LANES] for x in (panel_a, panel_n))
        own[2 * pair] = pack(a, n)
        own[2 * pair + 1] = jnp.where(low_lanes(a.shape), swap_halves(a), n)
    pl.semaphore_wait(barrier, 2 * STRIDE + (NC - 1) + (NP - 1))

    def along(d, hops):
        return lax.rem(u + (hops if d == 0 else NR - hops), NR)

    def slot(d, hops):
        return min(2 * hops - 1 + d, NR - 1)

    def arrived(buf, sem):
        remote(buf, buf, tile_send, sem, (u, mate, p)).wait_recv()

    def left(buf, sem):
        remote(buf, buf, sem, g_recv, (u, mate, p)).wait_send()

    for step in (1, 2, 6, 3, 7, 4, 5):
        to = lax.rem(v + step, NC)
        back = tile_recv.at[lax.rem(chip + CHIPS - to // 2, CHIPS)]
        remote(own.at[to], zbuf.at[0, v], tile_send, back, (u, to, p)).start()
    zbuf[0, v] = own[v]
    rows[v] = own[...]
    later[0].wait()
    for step in (2, 6):
        remote(gt.at[v], gt.at[v], g_send, g_recv, (u, lax.rem(v + step, NC), p)).start()
    remote(gt.at[v], gt.at[v], g_send, g_pass, (u, mate, p)).start()
    for step in (2, 6):
        remote(own, rows.at[v], r_send, r_recv, (u, lax.rem(v + step, NC), p)).start()
    remote(own, rows.at[v], r_send, r_pass, (u, mate, p)).start()

    def tiles(k):
        return pl.ds(2 * lax.rem(chip + k, CHIPS), 2)

    for k in NEAREST:
        arrived(zbuf.at[0, : 2 if k else 1], tile_recv.at[k])
        for hops in (STRIDE, 1):
            for d in range(2):
                sem = z_rest.at[k] if hops == 1 else z_pass.at[d, 0, k]
                to = (along(d, hops), v, p)
                remote(zbuf.at[0, tiles(k)], zbuf.at[slot(d, hops), tiles(k)], z_send, sem, to).start()

    for copy in later[1:]:
        copy.wait()
    scale = weight * (u < NP).astype(F32)
    inner = dot(dbk[...], coup[:, lanes])
    inner = jnp.where(h == 0, inner, swap_halves(inner)) * scale
    fixed[...] = dot(coup[pl.ds(part * CHUNK, CHUNK), :], inner, ((0,), (0,)))
    block = jnp.where(h == 0, dak[...], swap_halves(dak[...])) * scale
    fixed[pl.ds(part * CHUNK, CHUNK)] += block

    def relay(level):
        past = STRIDE * (level + 1)
        for k in NEAREST:
            for d in range(2):
                here = zbuf.at[slot(d, past), tiles(k)]
                arrived(here, z_pass.at[d, level, k])
                for more in (2, 1):
                    hops = past + more
                    if hops <= REACH[d][k % 2]:
                        sem = z_pass.at[d, 1, k] if hops == 4 else z_rest.at[k]
                        there = zbuf.at[slot(d, hops), tiles(k)]
                        remote(here, there, z_send, sem, (along(d, more), v, p)).start()

    def across(buf, send, recv, onward, final):
        arrived(buf.at[:2], recv)
        size = buf.shape[1] // 2
        for half, (source, to) in enumerate(((6, 2), (2, 6))):
            source = lax.rem(v + source, NC)
            block = buf.at[source, pl.ds(half * size, size)]
            remote(block, block, send, onward, (u, lax.rem(v + to, NC), p)).start()
            remote(buf.at[source], buf.at[source], send, final, (u, mate, p)).start()

    def opposite(buf, send, onward, final):
        block = buf.at[lax.rem(v + 4, NC)]
        arrived(block, onward)
        remote(block, block, send, final, (u, mate, p)).start()

    relay(0)
    across(gt, g_send, g_recv, g_opp, g_pass)
    across(rows, r_send, r_recv, r_opp, r_pass)
    relay(1)

    def share(k):
        parts = []
        for r in range(NR):
            origin = along(r % 2, (r + 1) // 2)
            at = pl.ds(pl.multiple_of(origin * BLOCK, BLOCK), BLOCK)
            parts.append(gt[tiles(k), at].reshape(2 * BLOCK, ROWS))
        inverse[k] = jnp.concatenate(parts, axis=0).T

    def column_sum(k):
        arrived(zbuf.at[: NR // 2 + 1, :2], z_rest.at[k])
        return dot(inverse[k], zbuf[:, tiles(k)].reshape(2 * NR * BLOCK, LANES))

    arrived(gt.at[:3], g_pass)
    for k in NEAREST[:3]:
        share(k)
    opposite(gt, g_send, g_opp, g_last)
    opposite(rows, r_send, r_opp, r_pass)
    both = column_sum(NEAREST[0])
    for k in NEAREST[1:3]:
        both = both + column_sum(k)
    arrived(gt.at[0], g_last)
    share(NEAREST[3])
    both = both + column_sum(NEAREST[3])
    arrived(rows.at[:4], r_pass)
    for a in range(NP):
        high, low = halves(rows[:, a].reshape(ROWS, LANES).T)
        turned[a * LANES : (a + 1) * LANES, :ROWS] = high
        turned[a * LANES : (a + 1) * LANES, ROWS:] = low

    panel = ((swap_halves(both) - both) * weight).reshape(NC, BLOCK, LANES)
    panel_out[...] = pack(panel[:, : BLOCK // 2], panel[:, BLOCK // 2 :])
    high, low = halves(both * weight)
    right = jnp.concatenate([high, low], axis=1)
    right = jnp.concatenate([right, jnp.concatenate([high, jnp.zeros_like(low)], axis=1)], axis=0)
    half = NP // 2
    for part in range(2):
        begin = half * lax.rem(v // half + 1 + part, 2)
        lhs = turned[pl.ds(pl.multiple_of(begin * LANES, half * LANES), half * LANES)]
        out = lax.dot_general(lhs, right, (((1,), (0,)), ((), ())), preferred_element_type=F32)
        out = (out[:, :LANES] + out[:, LANES:]).reshape(half, LANES, LANES)
        for k in range(half):
            a, top = begin + k, out[k, :CHUNK]
            qsend[a] = jnp.where(low_lanes((HALF, LANES)), swap_halves(top[:HALF]), top[HALF:])
            to_me = jnp.logical_and(v == p, a == v)

            @pl.when(to_me)
            def _():
                qrecv[p] = qsend[a]

            @pl.when(jnp.logical_not(to_me))
            def _():
                remote(qsend.at[a], qrecv.at[p], q_send, q_recv, (u, a, v)).start()

        for k in range(half):
            a, top, bottom = begin + k, out[k, :CHUNK], out[k, CHUNK:]
            own_part = fixed[pl.ds(pl.multiple_of(a * CHUNK, CHUNK), CHUNK)]
            first = top + swap_halves(bottom - top) + own_part
            fsend[a] = pack(first[:HALF], first[HALF:])

    frecv[p] = fsend[p]
    for step in range(1, NP):
        a = lax.rem(p + step, NP)
        remote(fsend.at[a], frecv.at[p], f_send, f_recv, (u, v, a)).start()
    for a in range(NC):
        to_me = jnp.logical_and(v == p, a == v)

        @pl.when(to_me)
        def _():
            panel_in[p] = panel_out[a]

        @pl.when(jnp.logical_not(to_me))
        def _():
            remote(panel_out.at[a], panel_in.at[p], n_send, n_recv, (u, a, v)).start()

    arrived(frecv.at[: NP - 1], f_recv)

    @pl.when(v == p)
    def _():
        arrived(qrecv.at[: NP - 1], q_recv)

    @pl.when(v != p)
    def _():
        arrived(qrecv, q_recv)

    first, second = frecv[0], qrecv[0]
    for q in range(1, NP):
        first, second = first + frecv[q], second + qrecv[q]
    back = unpack(second)
    back = jnp.concatenate([back, back], axis=0).T[:CHUNK]
    total = unpack(first) - back
    tsend[...] = pack(total[:HALF], total[HALF:])
    for step in FAR_FIRST:
        to = lax.rem(u + step, NR)
        remote(tsend, trecv.at[u], t_send, t_recv, (to, v, p)).start()
    trecv[u] = tsend[...]

    @pl.when(v == p)
    def _():
        arrived(panel_in.at[: NP - 1], n_recv)

    @pl.when(v != p)
    def _():
        arrived(panel_in, n_recv)

    total = panel_in[0]
    for k in range(1, NP):
        total = total + panel_in[k]
    panel_ref[...] = unpack(total)[:, :CHUNK]

    arrived(trecv.at[: NR - 1], t_recv)
    total = trecv[0]
    for k in range(1, NR):
        total = total + trecv[k]
    diag_ref[...] = unpack(total)[:, :CHUNK]

    left(own.at[: NC - 1], tile_send)
    left(gt.at[: NC - 1], g_send)
    left(rows.at[: NC - 1], r_send)
    left(zbuf.at[: NR - 1], z_send)
    left(fsend.at[: NP - 1], f_send)
    left(trecv.at[: NR - 1], t_send)

    @pl.when(v == p)
    def _():
        left(qsend.at[: NP - 1], q_send)
        left(panel_out.at[: NC - 1], n_send)

    @pl.when(v != p)
    def _():
        left(qsend, q_send)
        left(panel_out, n_send)


def shards(
    inverse_grid, factor_b, factor_a, coupling_a, diag_inv_b, diag_inv_a, pole_weights, structure
):
    hbm = pl.BlockSpec(memory_space=pltpu.HBM)
    vmem = pl.BlockSpec(memory_space=pltpu.VMEM)
    dma = pltpu.SemaphoreType.DMA
    panel, diag = pl.pallas_call(
        kernel,
        out_shape=(
            pltpu.VMEM((BLOCK, CHUNK), F32),
            pltpu.VMEM((CHUNK, CHUNK), F32),
        ),
        in_specs=[hbm] * 8,
        out_specs=(vmem, vmem),
        scratch_shapes=[
            pltpu.SMEM((1,), F32),
            pltpu.SMEM((2,), jnp.int32),
            pltpu.VMEM((NC, NR * BLOCK, ROWS), F32),
            pltpu.VMEM((BLOCK, WIDTH), F32),
            pltpu.VMEM((BLOCK, WIDTH), F32),
            pltpu.VMEM((WIDTH, WIDTH), F32),
            pltpu.VMEM((CHUNK, WIDTH), F32),
            pltpu.VMEM((CHUNK, LANES), F32),
            pltpu.VMEM((WIDTH, LANES), F32),
            pltpu.VMEM((NC, BLOCK, LANES), F32),
            pltpu.VMEM((NR, NC, BLOCK, LANES), F32),
            pltpu.VMEM((NC, NC, BLOCK, LANES), F32),
            pltpu.VMEM((CHIPS, ROWS, 2 * NR * BLOCK), F32),
            pltpu.VMEM((NP * LANES, 2 * ROWS), jnp.bfloat16),
            pltpu.VMEM((NC, BLOCK // 2, LANES), F32),
            pltpu.VMEM((NP, BLOCK // 2, LANES), F32),
            pltpu.VMEM((NP, HALF, LANES), F32),
            pltpu.VMEM((NP, HALF, LANES), F32),
            pltpu.VMEM((NP, HALF, LANES), F32),
            pltpu.VMEM((NP, HALF, LANES), F32),
            pltpu.VMEM((HALF, LANES), F32),
            pltpu.VMEM((NR, HALF, LANES), F32),
            dma((5,)), dma((3,)), dma, dma((NC // 2,)), dma, dma, dma, dma, dma, dma((2, 2, NC // 2)), dma((NC // 2,)), dma, dma,
            dma, dma, dma, dma, dma, dma, dma, dma, dma, dma, dma,
        ],
        compiler_params=pltpu.CompilerParams(collective_id=0, has_side_effects=True),
    )(
        inverse_grid[0, 0, :, 0, :].T,
        factor_b[0, 0, 0],
        factor_a[0, 0, 0],
        coupling_a[0],
        diag_inv_b[0],
        diag_inv_a[0],
        pole_weights,
        structure[:, 0, 0],
    )
    return panel[None, None], diag


def solution(mesh):
    in_specs = (
        P("poles", "rows", None, "cols", None),
        P("poles", "rows", "cols", None, None),
        P("poles", "rows", "cols", None, None),
        P("poles", None, None),
        P("poles", None, None),
        P("poles", None, None),
        P("poles"),
        P(None, "rows", "cols"),
    )
    out_specs = (P("rows", "cols", None, "poles"), P("poles", "cols"))
    return jax.shard_map(shards, mesh=mesh, in_specs=in_specs, out_specs=out_specs, check_vma=False)
```
